32 devices in a mesh: groups: 2 (over y), node: 4 (over z), feat: 4 (over x, core).
Axes of the slice: x: 2, y: 2, z: 4, core: 2. Of those that a mesh axis runs over, the one named last changes fastest.
Arguments:
- features: bfloat16 [12288, 256], P(('groups', 'node'), 'feat'), parts along dimension 0, may hold values from -6 to 6
- tiles: bfloat16 [96, 8, 128, 128], P(('groups', 'node')), parts along dimension 0, may hold values from 0 to 0.0625
- col_block: int32 [96, 8], P(('groups', 'node')), parts along dimension 0, may hold values from 0 to 47, as said below
- weight: bfloat16 [256, 172], replicated, may hold values from -0.375 to 0.375
- bias: float32 [172], replicated, may hold values from -1 to 1
Outputs:
- logits: bfloat16 [12288, 172], P(('groups', 'node', 'feat')), parts along dimension 0
The draws below stay inside these ranges and needn't reach their ends.
There are 2 independent parts, one for each index of `groups`. The reference program is written for one: setup_inputs(seed, part) draws one part's arguments, and reference() takes and returns one part's arrays. A program takes and returns all parts, laid end to end along the dimension named above; an argument that names none is the same for every part. Nothing has to cross between parts.
Inputs may be any that keep to these rules, and one draw needn't show every extreme that they name: `col_block`: stripe d holds block rows d * 12 to (d + 1) * 12 - 1. Slot 0 of block row r is r itself; every other slot names a block of another stripe. Over the block rows of one stripe, at most 28 slots name blocks of any one other stripe, and exactly 28 name blocks of some other stripe. The same block may be named more than once.
All inputs are finite; a program needn't handle non-finite values.
Results may differ from the reference program's by a relative error of at most 0.0046.
Values may be sent and summed in bfloat16 or wider, within the bound.
A program may use at most 128 MiB of HBM per device.

```python
import jax
import jax.numpy as jnp
from jax import lax

HID = 256
CLASSES = 172
BLOCK = 128
K = 8
SB = 12
NB = 48
NODES = 6144
REMOTE = 84
MAXB = 28
N_NODE = 4


def draw_col_block(key, part):

    def one_stripe(stripe):
        stripe_key = jax.random.fold_in(key, stripe + 7919)
        key_star, key_pool, key_order, key_local = jax.random.split(stripe_key, 4)
        star_offset = jax.random.randint(key_star, (), 1, N_NODE).astype(jnp.int32)
        pool_ids = jax.random.permutation(key_pool, (N_NODE - 2) * MAXB)[:REMOTE - MAXB].astype(jnp.int32)
        others = 1 + pool_ids // MAXB
        others = others + (others >= star_offset).astype(jnp.int32)
        offsets = jnp.concatenate([jnp.full((MAXB,), star_offset, jnp.int32), others.astype(jnp.int32)])
        offsets = offsets[jax.random.permutation(key_order, REMOTE)]
        local_ids = jax.random.randint(key_local, (REMOTE,), 0, SB).astype(jnp.int32)
        source = (stripe + offsets) % N_NODE
        remote = (source * SB + local_ids).reshape(SB, K - 1)
        diagonal = stripe * SB + jnp.arange(SB, dtype=jnp.int32)
        return jnp.concatenate([diagonal[:, None], remote], axis=1).astype(jnp.int32)
    stacked = jax.vmap(one_stripe)(jnp.arange(N_NODE, dtype=jnp.int32))
    return stacked.reshape(NB, K)


def level_of(key, shape, cuts, low, largest):
    factor_of = 1.0
    for axis_at, parts in cuts:
        heights = jax.random.uniform(jax.random.fold_in(jax.random.fold_in(key, 6), axis_at), (parts,), jnp.float32, low / len(cuts), largest / len(cuts))
        factor_of = factor_of * jnp.repeat(jnp.exp(heights), shape[axis_at] // parts).reshape((-1,) + (1,) * (len(shape) - 1 - axis_at))
    return factor_of


def scatter_about(own_key, extent, width, most, cuts=(), kind=jnp.bfloat16):
    values = jax.random.normal(own_key, extent, jnp.float32) * width
    if len(cuts) > 0:
        values = level_of(own_key, extent, cuts, -0.22, 0.18) * values
    return jnp.clip(values, min=-most, max=most).astype(kind)


def setup_inputs(seed: int = 0, part: int = 0) -> dict:
    splits = jax.random.split(jax.random.key(seed), 6)
    part_splits = jax.random.split(jax.random.fold_in(splits[5], part), 6)
    features = scatter_about(part_splits[0], (NODES, HID), 1.0, 6.0, ((0, 4), (1, 4)))
    tiles = jnp.clip(0.0625 * jax.random.uniform(part_splits[1], (NB, K, BLOCK, BLOCK), jnp.float32) ** level_of(part_splits[1], (NB, K, BLOCK, BLOCK), ((0, 4),), -0.2, 0.2), 0.0, 0.0625).astype(jnp.bfloat16)
    col_block = draw_col_block(jax.random.fold_in(jax.random.fold_in(splits[5], part), 71), part)
    weight = scatter_about(splits[3], (HID, CLASSES), HID ** -0.5, 0.375)
    bias = jnp.clip(jax.random.uniform(splits[4], (CLASSES,), jnp.float32, -1.0, 1.0), -1.0, 1.0)
    return dict(features=features, tiles=tiles, col_block=col_block, weight=weight, bias=bias)


def reference(features, tiles, col_block, weight, bias):
    blocks = features.reshape(NB, BLOCK, HID)

    def one_stripe(inputs):
        tile_rows, col_rows = inputs
        picked = blocks[col_rows.astype(jnp.int32)].astype(jnp.float32)
        summed = jnp.einsum("rkij,rkjf->rif", tile_rows.astype(jnp.float32), picked)
        return summed.astype(jnp.bfloat16)

    aggregated = lax.map(one_stripe, (tiles.reshape(N_NODE, SB, K, BLOCK, BLOCK), col_block.reshape(N_NODE, SB, K)))
    aggregated = aggregated.reshape(NODES, HID)
    logits = jnp.dot(aggregated, weight, preferred_element_type=jnp.float32) + bias
    return logits.astype(jnp.bfloat16)
```

```python
import functools

import jax
import jax.numpy as jnp
from jax import lax
from jax.experimental import pallas as pl
from jax.experimental.pallas import tpu as pltpu
from jax.sharding import PartitionSpec as P

MESH = pl.DeviceIdType.MESH
PHASES = ((0, 1), (2, 3))
PIECES = 4


def kernel(nodes, feats, cols_hbm, x, tiles_hbm, weight_hbm, bias_hbm, out, cols, weight, bias, column, tiles, agg, parts,
           full, own_sem, tile_sem, small_sem, right_send, right_recv, left_send, left_recv, ex_send, ex_recv, *held):
    node = lax.axis_index("node")
    feat = lax.axis_index("feat")
    width = x.shape[0]
    piece = width // PIECES
    block_rows, slots, block, _ = tiles.shape
    share = block_rows // feats
    span = share * block

    def stripe_of(p, stripe):
        return held[p].at[pl.ds(stripe * block_rows, block_rows)]

    for p in range(PIECES):
        for b in range(block_rows):
            pltpu.make_async_copy(
                x.at[pl.ds(p * piece, piece), pl.ds(b * block, block)],
                held[p].at[node * block_rows + b],
                own_sem.at[p],
            ).start()
    barrier = pltpu.get_barrier_semaphore()

    @pl.when(node > 0)
    def _():
        pl.semaphore_signal(barrier, inc=1, device_id={"node": node - 1}, device_id_type=MESH)

    @pl.when(node < nodes - 1)
    def _():
        pl.semaphore_signal(barrier, inc=1, device_id={"node": node + 1}, device_id_type=MESH)

    for k in range(1, feats):
        pl.semaphore_signal(
            barrier, inc=1, device_id={"feat": lax.rem(feat + k, feats)}, device_id_type=MESH
        )
    neighbours = jnp.where(node > 0, 1, 0) + jnp.where(node < nodes - 1, 1, 0)
    pl.semaphore_wait(barrier, neighbours + (feats - 1))

    def right(step, p):
        stripe = jnp.maximum(node - step, 0)
        return pltpu.make_async_remote_copy(
            stripe_of(p, stripe), stripe_of(p, stripe), right_send.at[step, p], right_recv.at[step, p],
            device_id={"node": jnp.minimum(node + 1, nodes - 1)}, device_id_type=MESH,
        )

    def left(step, p):
        stripe = jnp.minimum(node + step, nodes - 1)
        return pltpu.make_async_remote_copy(
            stripe_of(p, stripe), stripe_of(p, stripe), left_send.at[step, p], left_recv.at[step, p],
            device_id={"node": jnp.maximum(node - 1, 0)}, device_id_type=MESH,
        )

    def sends_right(step):
        return jnp.logical_and(node < nodes - 1, node >= step)

    def sends_left(step):
        return jnp.logical_and(node > 0, node + step <= nodes - 1)

    def takes_left(step):
        return node + 1 + step <= nodes - 1

    def takes_right(step):
        return node - 1 - step >= 0

    def send(step, p):
        if step == 0:
            own = stripe_of(p, node)
            pltpu.make_async_copy(own, own, own_sem.at[p]).wait()
        pl.when(sends_right(step))(lambda: right(step, p).start())
        pl.when(sends_left(step))(lambda: left(step, p).start())

    def take(step, p):
        pl.when(takes_right(step))(lambda: right(step, p).wait_recv())
        pl.when(takes_left(step))(lambda: left(step, p).wait_recv())

    def forward_phase(pieces):
        for step in range(1, nodes - 1):
            for p in pieces:
                take(step - 1, p)
                send(step, p)

    def finish_phase(pieces):
        for p in pieces:
            take(nodes - 2, p)

    def exchange(phase, k):
        pieces = PHASES[phase]
        height = piece * len(pieces)
        low = pieces[0] * piece
        peer = lax.rem(feat + k, feats)
        return pltpu.make_async_remote_copy(
            agg.at[pl.ds(low, height), pl.ds(pl.multiple_of(peer * span, span), span)],
            full[phase].at[pl.ds(pl.multiple_of(feat * height, height), height)],
            ex_send.at[phase, k], ex_recv.at[phase, k],
            device_id={"feat": peer}, device_id_type=MESH,
        )

    order = list(range(1, feats))
    if feats == 4:
        odd = lax.rem(feat, 2)
        order = [2, 3 - 2 * odd, 1 + 2 * odd]

    def aggregate(phase):
        pieces = PHASES[phase]
        height = piece * len(pieces)
        low = pieces[0] * piece
        for k in order + [0]:
            peer = lax.rem(feat + k, feats)
            sums = []
            for j in range(share):
                r = peer * share + j
                picked = [
                    jnp.concatenate([held[p][cols[s, r]] for p in pieces], axis=0)
                    for s in range(slots)
                ]
                sums.append(lax.dot_general(
                    jnp.concatenate([tiles[r, s] for s in range(slots)], axis=1),
                    jnp.concatenate(picked, axis=1),
                    (((1,), (1,)), ((), ())),
                    preferred_element_type=jnp.float32,
                ))
            rounded = jnp.concatenate([part.T for part in sums], axis=1).astype(jnp.bfloat16)
            if isinstance(k, int) and k == 0:
                here = pl.ds(pl.multiple_of(feat * height, height), height)
                full[phase][here, :] = rounded
            else:
                there = pl.ds(pl.multiple_of(peer * span, span), span)
                agg[pl.ds(low, height), there] = rounded
            if not (isinstance(k, int) and k == 0):
                exchange(phase, k).start()

    def project(phase):
        for k in range(1, feats):
            exchange(phase, k).wait_recv()
        return jnp.dot(parts[phase], full[phase][...], preferred_element_type=jnp.float32)

    for p in range(PIECES):
        send(0, p)
    tile_copy = pltpu.make_async_copy(tiles_hbm, tiles, tile_sem)
    tile_copy.start()
    cols_copy = pltpu.make_async_copy(cols_hbm, cols, small_sem.at[0])
    cols_copy.start()
    weight_copy = pltpu.make_async_copy(weight_hbm, weight, small_sem.at[1])
    weight_copy.start()
    bias_copy = pltpu.make_async_copy(bias_hbm, bias, small_sem.at[2])
    bias_copy.start()

    forward_phase(range(PIECES))
    weight_copy.wait()
    for phase, pieces in enumerate(PHASES):
        low, high = pieces[0] * piece, (pieces[-1] + 1) * piece
        parts[phase] = jnp.concatenate(
            [weight[:, f * width + low : f * width + high] for f in range(feats)], axis=1
        )
    bias_copy.wait()
    column[...] = jnp.broadcast_to(bias[...], (block, bias.shape[1])).T
    cols_copy.wait()
    tile_copy.wait()
    for phase, pieces in enumerate(PHASES):
        finish_phase(pieces)
        aggregate(phase)

    total = jnp.concatenate([column[...]] * share, axis=1)
    for phase in range(len(PHASES)):
        total += project(phase)
    out[...] = total.astype(out.dtype)

    for step in range(nodes - 1):
        for p in range(PIECES):
            pl.when(sends_right(step))(lambda: right(step, p).wait_send())
            pl.when(sends_left(step))(lambda: left(step, p).wait_send())
    for phase in range(len(PHASES)):
        for k in range(1, feats):
            exchange(phase, k).wait_send()


def on_device(nodes, feats, features, tiles, col_block, weight, bias):
    rows, width = features.shape
    block_rows, slots, block, _ = tiles.shape
    share = rows // feats
    phases = len(PHASES)
    classes = weight.shape[1]
    half = feats * width // phases
    logits = pl.pallas_call(
        functools.partial(kernel, nodes, feats),
        out_shape=pltpu.VMEM((classes, share), jnp.bfloat16),
        in_specs=[
            pl.BlockSpec(memory_space=pl.ANY),
            pl.BlockSpec(memory_space=pl.ANY),
            pl.BlockSpec(memory_space=pl.ANY),
            pl.BlockSpec(memory_space=pl.ANY),
            pl.BlockSpec(memory_space=pl.ANY),
        ],
        out_specs=pl.BlockSpec(memory_space=pltpu.VMEM),
        scratch_shapes=[
            pltpu.SMEM(col_block.shape[::-1], col_block.dtype),
            pltpu.VMEM(weight.shape[::-1], weight.dtype),
            pltpu.VMEM((1, classes), bias.dtype),
            pltpu.VMEM((classes, block), bias.dtype),
            pltpu.VMEM(tiles.shape, tiles.dtype),
            pltpu.VMEM((width, rows), features.dtype),
            pltpu.VMEM((phases, classes, half), weight.dtype),
            [pltpu.VMEM((half, share), features.dtype)] * phases,
            pltpu.SemaphoreType.DMA((PIECES,)),
            pltpu.SemaphoreType.DMA,
            pltpu.SemaphoreType.DMA((3,)),
            pltpu.SemaphoreType.DMA((nodes - 1, PIECES)),
            pltpu.SemaphoreType.DMA((nodes - 1, PIECES)),
            pltpu.SemaphoreType.DMA((nodes - 1, PIECES)),
            pltpu.SemaphoreType.DMA((nodes - 1, PIECES)),
            pltpu.SemaphoreType.DMA((phases, feats)),
            pltpu.SemaphoreType.DMA((phases, feats)),
            *[pltpu.VMEM((nodes * block_rows, width // PIECES, block), features.dtype)] * PIECES,
        ],
        compiler_params=pltpu.CompilerParams(collective_id=0, has_side_effects=True),
    )(col_block.T, features.T, tiles, weight.T, bias[None])
    return logits.T


def solution(mesh):
    in_specs = (
        P(("groups", "node"), "feat"),
        P(("groups", "node"), None, None, None),
        P(("groups", "node"), None),
        P(),
        P(),
    )
    out_specs = P(("groups", "node", "feat"), None)
    body = functools.partial(on_device, mesh.shape["node"], mesh.shape["feat"])
    return jax.shard_map(
        body, mesh=mesh, in_specs=in_specs, out_specs=out_specs, check_vma=False
    )
```

```python
import functools

import jax
import jax.numpy as jnp
from jax import lax
from jax.experimental import pallas as pl
from jax.experimental.pallas import tpu as pltpu
from jax.sharding import PartitionSpec as P

MESH = pl.DeviceIdType.MESH
PIECES = 4


def kernel(nodes, feats, cols_hbm, x, tiles_hbm, weight_hbm, bias_hbm, out, cols, weight, bias, column, tiles, agg, full, blocks, own_sem, tile_sem, small_sem, right_send, right_recv, left_send, left_recv,
           ex_send, ex_recv, right_in, above_in, feats_in, *held):
    node = lax.axis_index("node")
    feat = lax.axis_index("feat")
    odd = lax.rem(feat, 2)
    width = x.shape[0]
    piece = width // PIECES
    block_rows, slots, block, _ = tiles.shape
    share = block_rows // feats
    span = share * block
    stripe_rows = block_rows * block
    peers = [lax.rem(feat + k, feats) for k in range(1, feats)]

    barrier = pltpu.get_barrier_semaphore()

    @pl.when(node < nodes - 1)
    def _():
        pl.semaphore_signal(barrier, inc=1, device_id={"node": node + 1}, device_id_type=MESH)

    @pl.when(node == 0)
    def _():
        for peer in peers:
            pl.semaphore_signal(barrier, inc=1, device_id={"feat": peer}, device_id_type=MESH)

    pl.semaphore_wait(barrier, jnp.where(node == 0, feats - 1, 1))

    @pl.when(node > 0)
    def _():
        pl.semaphore_signal(right_in, inc=1, device_id={"node": node - 1}, device_id_type=MESH)

    def meet():
        @pl.when(node > 0)
        def _():
            pl.semaphore_wait(feats_in, 1)

        @pl.when(node < nodes - 1)
        def _():
            for peer in peers:
                pl.semaphore_signal(above_in, inc=1, device_id={"feat": peer}, device_id_type=MESH)
            pl.semaphore_wait(above_in, feats - 1)
            pl.semaphore_signal(feats_in, inc=1, device_id={"node": node + 1}, device_id_type=MESH)

    def stripe_of(p, stripe):
        return held[p].at[:, pl.ds(pl.multiple_of(stripe * stripe_rows, stripe_rows), stripe_rows)]

    def source(step, p, stripe):
        return x.at[pl.ds(p * piece, piece)] if step == 0 else stripe_of(p, stripe)

    def right(step, p):
        stripe = jnp.maximum(node - step, 0)
        return pltpu.make_async_remote_copy(
            source(step, p, stripe), stripe_of(p, stripe), right_send.at[step, p], right_recv.at[step, p],
            device_id={"node": jnp.minimum(node + 1, nodes - 1)}, device_id_type=MESH,
        )

    def left(step, p):
        stripe = jnp.minimum(node + step, nodes - 1)
        return pltpu.make_async_remote_copy(
            source(step, p, stripe), stripe_of(p, stripe), left_send.at[step, p], left_recv.at[step, p],
            device_id={"node": jnp.maximum(node - 1, 0)}, device_id_type=MESH,
        )

    def sends_right(step):
        return jnp.logical_and(node < nodes - 1, node >= step)

    def sends_left(step):
        return jnp.logical_and(node > 0, node + step <= nodes - 1)

    def takes_left(step):
        return node + 1 + step <= nodes - 1

    def takes_right(step):
        return node - 1 - step >= 0

    def send(step, p):
        pl.when(sends_right(step))(lambda: right(step, p).start())
        pl.when(sends_left(step))(lambda: left(step, p).start())

    def take(step, p):
        pl.when(takes_right(step))(lambda: right(step, p).wait_recv())
        pl.when(takes_left(step))(lambda: left(step, p).wait_recv())

    def unpack_stripe(p, stripe):
        def one(b, carry):
            at = pl.multiple_of(stripe * stripe_rows + b * block, block)
            blocks[stripe * block_rows + b, p * piece:(p + 1) * piece, :] = held[p][:, pl.ds(at, block)]
            return carry

        lax.fori_loop(0, block_rows, one, 0, unroll=False)

    def unpack(step, p):
        pl.when(takes_right(step))(lambda: unpack_stripe(p, node - 1 - step))
        pl.when(takes_left(step))(lambda: unpack_stripe(p, node + 1 + step))

    order = list(range(1, feats))
    if feats == 4:
        order = [2 - odd, 3 - odd, 1 + 2 * odd]

    def exchange(k):
        peer = lax.rem(feat + k, feats)
        return pltpu.make_async_remote_copy(
            agg.at[:, pl.ds(pl.multiple_of(peer * span, span), span)],
            full.at[pl.ds(pl.multiple_of(feat * width, width), width)],
            ex_send.at[k], ex_recv.at[k], device_id={"feat": peer}, device_id_type=MESH,
        )

    def aggregate(i, carry):
        k = jnp.int32(0)
        for at, step in enumerate(order):
            k = jnp.where(i == at, step, k)
        peer = lax.rem(feat + k, feats)
        sums = []
        for j in range(share):
            r = peer * share + j
            sums.append(lax.dot_general(
                jnp.concatenate([blocks[cols[s, r]] for s in range(slots)], axis=1),
                jnp.concatenate([tiles[r, s] for s in range(slots)], axis=1),
                (((1,), (1,)), ((), ())),
                preferred_element_type=jnp.float32,
            ))
        rounded = jnp.concatenate(sums, axis=1).astype(jnp.bfloat16)
        agg[:, pl.ds(pl.multiple_of(peer * span, span), span)] = rounded

        @pl.when(i < feats - 1)
        def _():
            exchange(k).start()

        return carry

    for p in range(PIECES):
        pl.when(sends_left(0))(lambda: left(0, p).start())

    @pl.when(node < nodes - 1)
    def _():
        pl.semaphore_wait(right_in, 1)

    for p in range(PIECES):
        pl.when(sends_right(0))(lambda: right(0, p).start())
    own = [pltpu.make_async_copy(source(0, p, node), stripe_of(p, node), own_sem.at[p]) for p in range(PIECES)]
    for copy in own:
        copy.start()
    weight_copy = pltpu.make_async_copy(weight_hbm, weight, small_sem.at[1])
    weight_copy.start()
    bias_copy = pltpu.make_async_copy(bias_hbm, bias, small_sem.at[2])
    bias_copy.start()
    cols_copy = pltpu.make_async_copy(cols_hbm, cols, small_sem.at[0])
    cols_copy.start()
    tile_copy = pltpu.make_async_copy(tiles_hbm, tiles, tile_sem)
    tile_copy.start()

    pl.when(node <= 1)(meet)
    weight_copy.wait()
    bias_copy.wait()
    column[...] = jnp.broadcast_to(bias[...], (block, bias.shape[1])).T
    for step in range(1, nodes - 1):
        for p in range(PIECES):
            take(step - 1, p)
            send(step, p)
    pl.when(node > 1)(meet)
    for p in range(PIECES):
        own[p].wait()
        unpack_stripe(p, node)
    for step in range(nodes - 2):
        for p in range(PIECES):
            unpack(step, p)
    cols_copy.wait()
    tile_copy.wait()
    for p in range(PIECES):
        take(nodes - 2, p)
        unpack(nodes - 2, p)

    lax.fori_loop(0, feats, aggregate, 0)

    here = pl.ds(pl.multiple_of(feat * span, span), span)
    full[pl.ds(pl.multiple_of(feat * width, width), width), :] = agg[:, here]

    total = jnp.concatenate([column[...]] * share, axis=1)
    for k in range(1, feats):
        exchange(k).wait_recv()
    total += jnp.dot(weight[...], full[...], preferred_element_type=jnp.float32)
    out[...] = total.astype(out.dtype)

    for step in range(nodes - 1):
        for p in range(PIECES):
            pl.when(sends_right(step))(lambda: right(step, p).wait_send())
            pl.when(sends_left(step))(lambda: left(step, p).wait_send())
    for k in range(1, feats):
        exchange(k).wait_send()


def on_device(nodes, feats, features, tiles, col_block, weight, bias):
    rows, width = features.shape
    block_rows, _, block, _ = tiles.shape
    share = rows // feats
    classes = weight.shape[1]
    piece = width // PIECES
    logits = pl.pallas_call(
        functools.partial(kernel, nodes, feats),
        out_shape=pltpu.VMEM((classes, share), jnp.bfloat16),
        in_specs=[
            pl.BlockSpec(memory_space=pl.ANY),
            pl.BlockSpec(memory_space=pl.ANY),
            pl.BlockSpec(memory_space=pl.ANY),
            pl.BlockSpec(memory_space=pl.ANY),
            pl.BlockSpec(memory_space=pl.ANY),
        ],
        out_specs=pl.BlockSpec(memory_space=pltpu.VMEM),
        scratch_shapes=[
            pltpu.SMEM(col_block.shape[::-1], col_block.dtype),
            pltpu.VMEM(weight.shape[::-1], weight.dtype),
            pltpu.VMEM((1, classes), bias.dtype),
            pltpu.VMEM((classes, block), bias.dtype),
            pltpu.VMEM(tiles.shape, tiles.dtype),
            pltpu.VMEM((width, rows), features.dtype),
            pltpu.VMEM((feats * width, share), features.dtype),
            pltpu.VMEM((nodes * block_rows, width, block), features.dtype),
            pltpu.SemaphoreType.DMA((PIECES,)),
            pltpu.SemaphoreType.DMA,
            pltpu.SemaphoreType.DMA((3,)),
            pltpu.SemaphoreType.DMA((nodes - 1, PIECES)),
            pltpu.SemaphoreType.DMA((nodes - 1, PIECES)),
            pltpu.SemaphoreType.DMA((nodes - 1, PIECES)),
            pltpu.SemaphoreType.DMA((nodes - 1, PIECES)),
            pltpu.SemaphoreType.DMA((feats,)),
            pltpu.SemaphoreType.DMA((feats,)),
            pltpu.SemaphoreType.REGULAR,
            pltpu.SemaphoreType.REGULAR,
            pltpu.SemaphoreType.REGULAR,
            *[pltpu.VMEM((piece, nodes * rows), features.dtype)] * PIECES,
        ],
        compiler_params=pltpu.CompilerParams(collective_id=0, has_side_effects=True),
    )(col_block.T, features.T, tiles, weight.T, bias[None])
    return logits.T


def solution(mesh):
    in_specs = (
        P(("groups", "node"), "feat"),
        P(("groups", "node"), None, None, None),
        P(("groups", "node"), None),
        P(),
        P(),
    )
    out_specs = P(("groups", "node", "feat"), None)
    body = functools.partial(on_device, mesh.shape["node"], mesh.shape["feat"])
    return jax.shard_map(
        body, mesh=mesh, in_specs=in_specs, out_specs=out_specs, check_vma=False
    )
```

```python
import functools

import jax
import jax.numpy as jnp
from jax import lax
from jax.experimental import pallas as pl
from jax.experimental.pallas import tpu as pltpu
from jax.sharding import PartitionSpec as P

MESH = pl.DeviceIdType.MESH
PIECES = 4
LAG = 0


def kernel(nodes, feats, cols_hbm, x, tiles_hbm, weight_hbm, bias_hbm, out, cols, weight, bias, column, tiles, agg, full, blocks, own_sem, tile_sem, small_sem, right_send, right_recv, left_send, left_recv,
           ex_send, ex_recv, right_in, above_in, feats_in, *held):
    node = lax.axis_index("node")
    feat = lax.axis_index("feat")
    odd = lax.rem(feat, 2)
    width = x.shape[0]
    piece = width // PIECES
    block_rows, slots, block, _ = tiles.shape
    share = block_rows // feats
    span = share * block
    stripe_rows = block_rows * block
    peers = [lax.rem(feat + k, feats) for k in range(1, feats)]

    barrier = pltpu.get_barrier_semaphore()

    @pl.when(node < nodes - 1)
    def _():
        pl.semaphore_signal(barrier, inc=1, device_id={"node": node + 1}, device_id_type=MESH)

    @pl.when(node == 0)
    def _():
        for peer in peers:
            pl.semaphore_signal(barrier, inc=1, device_id={"feat": peer}, device_id_type=MESH)

    pl.semaphore_wait(barrier, jnp.where(node == 0, feats - 1, 1))

    @pl.when(node > 0)
    def _():
        pl.semaphore_signal(right_in, inc=1, device_id={"node": node - 1}, device_id_type=MESH)

    def meet():
        @pl.when(node > 0)
        def _():
            pl.semaphore_wait(feats_in, 1)

        @pl.when(node < nodes - 1)
        def _():
            for peer in peers:
                pl.semaphore_signal(above_in, inc=1, device_id={"feat": peer}, device_id_type=MESH)
            pl.semaphore_wait(above_in, feats - 1)
            pl.semaphore_signal(feats_in, inc=1, device_id={"node": node + 1}, device_id_type=MESH)

    def stripe_of(p, stripe):
        return held[p].at[:, pl.ds(pl.multiple_of(stripe * stripe_rows, stripe_rows), stripe_rows)]

    def source(step, p, stripe):
        return x.at[pl.ds(p * piece, piece)] if step == 0 else stripe_of(p, stripe)

    def right(step, p):
        stripe = jnp.maximum(node - step, 0)
        return pltpu.make_async_remote_copy(
            source(step, p, stripe), stripe_of(p, stripe), right_send.at[step, p], right_recv.at[step, p],
            device_id={"node": jnp.minimum(node + 1, nodes - 1)}, device_id_type=MESH,
        )

    def left(step, p):
        stripe = jnp.minimum(node + step, nodes - 1)
        return pltpu.make_async_remote_copy(
            source(step, p, stripe), stripe_of(p, stripe), left_send.at[step, p], left_recv.at[step, p],
            device_id={"node": jnp.maximum(node - 1, 0)}, device_id_type=MESH,
        )

    def sends_right(step):
        return jnp.logical_and(node < nodes - 1, node >= step)

    def sends_left(step):
        return jnp.logical_and(node > 0, node + step <= nodes - 1)

    def takes_left(step):
        return node + 1 + step <= nodes - 1

    def takes_right(step):
        return node - 1 - step >= 0

    def take(step, p):
        pl.when(takes_right(step))(lambda: right(step, p).wait_recv())
        pl.when(takes_left(step))(lambda: left(step, p).wait_recv())

    def unpack_stripe(p, stripe):
        def one(b, carry):
            at = pl.multiple_of(stripe * stripe_rows + b * block, block)
            blocks[stripe * block_rows + b, p * piece:(p + 1) * piece, :] = held[p][:, pl.ds(at, block)]
            return carry

        lax.fori_loop(0, block_rows, one, 0, unroll=False)

    def unpack(step, p):
        pl.when(takes_right(step))(lambda: unpack_stripe(p, node - 1 - step))
        pl.when(takes_left(step))(lambda: unpack_stripe(p, node + 1 + step))

    order = list(range(1, feats))
    if feats == 4:
        order = [2 - odd, 3 - odd, 1 + 2 * odd]

    def exchange(k):
        peer = lax.rem(feat + k, feats)
        return pltpu.make_async_remote_copy(
            agg.at[:, pl.ds(pl.multiple_of(peer * span, span), span)],
            full.at[pl.ds(pl.multiple_of(feat * width, width), width)],
            ex_send.at[k], ex_recv.at[k], device_id={"feat": peer}, device_id_type=MESH,
        )

    def aggregate(i, carry):
        k = jnp.int32(0)
        for at, step in enumerate(order):
            k = jnp.where(i == at, step, k)
        peer = lax.rem(feat + k, feats)
        sums = []
        for j in range(share):
            r = peer * share + j
            sums.append(lax.dot_general(
                jnp.concatenate([blocks[cols[s, r]] for s in range(slots)], axis=1),
                jnp.concatenate([tiles[r, s] for s in range(slots)], axis=1),
                (((1,), (1,)), ((), ())),
                preferred_element_type=jnp.float32,
            ))
        rounded = jnp.concatenate(sums, axis=1).astype(jnp.bfloat16)
        agg[:, pl.ds(pl.multiple_of(peer * span, span), span)] = rounded

        @pl.when(i < feats - 1)
        def _():
            exchange(k).start()

        return carry

    @pl.when(sends_left(0))
    def _():
        for p in range(PIECES):
            left(0, p).start()


    @pl.when(node < nodes - 1)
    def _():
        pl.semaphore_wait(right_in, 1)
        for p in range(PIECES):
            right(0, p).start()

    own = [pltpu.make_async_copy(source(0, p, node), stripe_of(p, node), own_sem.at[p]) for p in range(PIECES)]
    for copy in own:
        copy.start()
    weight_copy = pltpu.make_async_copy(weight_hbm, weight, small_sem.at[1])
    weight_copy.start()
    bias_copy = pltpu.make_async_copy(bias_hbm, bias, small_sem.at[2])
    bias_copy.start()
    cols_copy = pltpu.make_async_copy(cols_hbm, cols, small_sem.at[0])
    cols_copy.start()
    tile_copy = pltpu.make_async_copy(tiles_hbm, tiles, tile_sem)
    tile_copy.start()

    pl.when(node == 0)(meet)
    turns = [(step, p) for step in range(1, nodes - 1) for p in range(PIECES)]
    for at in range(len(turns) + LAG):
        if at < len(turns):
            step, p = turns[at]
            pl.when(takes_left(step - 1))(lambda: left(step - 1, p).wait_recv())
            pl.when(sends_left(step))(lambda: left(step, p).start())
        if at >= LAG:
            step, p = turns[at - LAG]
            pl.when(takes_right(step - 1))(lambda: right(step - 1, p).wait_recv())
            pl.when(sends_right(step))(lambda: right(step, p).start())
    pl.when(node > 0)(meet)
    weight_copy.wait()
    bias_copy.wait()
    column[...] = jnp.broadcast_to(bias[...], (block, bias.shape[1])).T
    for p in range(PIECES):
        own[p].wait()
        unpack_stripe(p, node)
    for step in range(nodes - 2):
        for taken, stripe in ((takes_right(step), node - 1 - step), (takes_left(step), node + 1 + step)):
            @pl.when(taken)
            def _():
                for p in range(PIECES):
                    unpack_stripe(p, stripe)

    cols_copy.wait()
    tile_copy.wait()
    for p in range(PIECES):
        take(nodes - 2, p)
        unpack(nodes - 2, p)

    lax.fori_loop(0, feats, aggregate, 0)

    here = pl.ds(pl.multiple_of(feat * span, span), span)
    full[pl.ds(pl.multiple_of(feat * width, width), width), :] = agg[:, here]

    for step in range(nodes - 1):
        @pl.when(sends_right(step))
        def _():
            for p in range(PIECES):
                right(step, p).wait_send()

        @pl.when(sends_left(step))
        def _():
            for p in range(PIECES):
                left(step, p).wait_send()

    total = jnp.concatenate([column[...]] * share, axis=1)
    for k in range(1, feats):
        exchange(k).wait_recv()
    total += jnp.dot(weight[...], full[...], preferred_element_type=jnp.float32)
    out[...] = total.astype(out.dtype)

    for k in range(1, feats):
        exchange(k).wait_send()


def on_device(nodes, feats, features, tiles, col_block, weight, bias):
    rows, width = features.shape
    block_rows, _, block, _ = tiles.shape
    share = rows // feats
    classes = weight.shape[1]
    piece = width // PIECES
    logits = pl.pallas_call(
        functools.partial(kernel, nodes, feats),
        out_shape=pltpu.VMEM((classes, share), jnp.bfloat16),
        in_specs=[
            pl.BlockSpec(memory_space=pl.ANY),
            pl.BlockSpec(memory_space=pl.ANY),
            pl.BlockSpec(memory_space=pl.ANY),
            pl.BlockSpec(memory_space=pl.ANY),
            pl.BlockSpec(memory_space=pl.ANY),
        ],
        out_specs=pl.BlockSpec(memory_space=pltpu.VMEM),
        scratch_shapes=[
            pltpu.SMEM(col_block.shape[::-1], col_block.dtype),
            pltpu.VMEM(weight.shape[::-1], weight.dtype),
            pltpu.VMEM((1, classes), bias.dtype),
            pltpu.VMEM((classes, block), bias.dtype),
            pltpu.VMEM(tiles.shape, tiles.dtype),
            pltpu.VMEM((width, rows), features.dtype),
            pltpu.VMEM((feats * width, share), features.dtype),
            pltpu.VMEM((nodes * block_rows, width, block), features.dtype),
            pltpu.SemaphoreType.DMA((PIECES,)),
            pltpu.SemaphoreType.DMA,
            pltpu.SemaphoreType.DMA((3,)),
            pltpu.SemaphoreType.DMA((nodes - 1, PIECES)),
            pltpu.SemaphoreType.DMA((nodes - 1, PIECES)),
            pltpu.SemaphoreType.DMA((nodes - 1, PIECES)),
            pltpu.SemaphoreType.DMA((nodes - 1, PIECES)),
            pltpu.SemaphoreType.DMA((feats,)),
            pltpu.SemaphoreType.DMA((feats,)),
            pltpu.SemaphoreType.REGULAR,
            pltpu.SemaphoreType.REGULAR,
            pltpu.SemaphoreType.REGULAR,
            *[pltpu.VMEM((piece, nodes * rows), features.dtype)] * PIECES,
        ],
        compiler_params=pltpu.CompilerParams(collective_id=0, has_side_effects=True),
    )(col_block.T, features.T, tiles, weight.T, bias[None])
    return logits.T


def solution(mesh):
    in_specs = (
        P(("groups", "node"), "feat"),
        P(("groups", "node"), None, None, None),
        P(("groups", "node"), None),
        P(),
        P(),
    )
    out_specs = P(("groups", "node", "feat"), None)
    body = functools.partial(on_device, mesh.shape["node"], mesh.shape["feat"])
    return jax.shard_map(
        body, mesh=mesh, in_specs=in_specs, out_specs=out_specs, check_vma=False
    )
```

```python
import functools

import jax
import jax.numpy as jnp
from jax import lax
from jax.experimental import pallas as pl
from jax.experimental.pallas import tpu as pltpu
from jax.sharding import PartitionSpec as P

MESH = pl.DeviceIdType.MESH
PIECES = 4
EARLY = 2


def kernel(nodes, feats, cols_hbm, x, tiles_hbm, weight_hbm, bias_hbm, out, cols, weight, bias, column, tiles, agg, full, blocks, own_sem, tile_sem, small_sem, right_send, right_recv, left_send, left_recv,
           ex_send, ex_recv, right_in, above_in, feats_in, *held):
    node = lax.axis_index("node")
    feat = lax.axis_index("feat")
    odd = lax.rem(feat, 2)
    width = x.shape[0]
    piece = width // PIECES
    block_rows, slots, block, _ = tiles.shape
    share = block_rows // feats
    span = share * block
    stripe_rows = block_rows * block
    peers = [lax.rem(feat + k, feats) for k in range(1, feats)]

    barrier = pltpu.get_barrier_semaphore()

    @pl.when(node < nodes - 1)
    def _():
        pl.semaphore_signal(barrier, inc=1, device_id={"node": node + 1}, device_id_type=MESH)

    @pl.when(node == 0)
    def _():
        for peer in peers:
            pl.semaphore_signal(barrier, inc=1, device_id={"feat": peer}, device_id_type=MESH)

    pl.semaphore_wait(barrier, jnp.where(node == 0, feats - 1, 1))

    @pl.when(node > 0)
    def _():
        pl.semaphore_signal(right_in, inc=1, device_id={"node": node - 1}, device_id_type=MESH)

    def meet():
        @pl.when(node > 0)
        def _():
            pl.semaphore_wait(feats_in, 1)

        @pl.when(node < nodes - 1)
        def _():
            for peer in peers:
                pl.semaphore_signal(above_in, inc=1, device_id={"feat": peer}, device_id_type=MESH)
            pl.semaphore_wait(above_in, feats - 1)
            pl.semaphore_signal(feats_in, inc=1, device_id={"node": node + 1}, device_id_type=MESH)

    def stripe_of(p, stripe):
        return held[p].at[:, pl.ds(pl.multiple_of(stripe * stripe_rows, stripe_rows), stripe_rows)]

    def source(step, p, stripe):
        return x.at[pl.ds(p * piece, piece)] if step == 0 else stripe_of(p, stripe)

    def right(step, p):
        stripe = jnp.maximum(node - step, 0)
        return pltpu.make_async_remote_copy(
            source(step, p, stripe), stripe_of(p, stripe), right_send.at[step, p], right_recv.at[step, p],
            device_id={"node": jnp.minimum(node + 1, nodes - 1)}, device_id_type=MESH,
        )

    def left(step, p):
        stripe = jnp.minimum(node + step, nodes - 1)
        return pltpu.make_async_remote_copy(
            source(step, p, stripe), stripe_of(p, stripe), left_send.at[step, p], left_recv.at[step, p],
            device_id={"node": jnp.maximum(node - 1, 0)}, device_id_type=MESH,
        )

    def sends_right(step):
        return jnp.logical_and(node < nodes - 1, node >= step)

    def sends_left(step):
        return jnp.logical_and(node > 0, node + step <= nodes - 1)

    def takes_left(step):
        return node + 1 + step <= nodes - 1

    def takes_right(step):
        return node - 1 - step >= 0

    def take(step, p):
        pl.when(takes_right(step))(lambda: right(step, p).wait_recv())
        pl.when(takes_left(step))(lambda: left(step, p).wait_recv())

    def unpack_stripe(p, stripe):
        def one(b, carry):
            at = pl.multiple_of(stripe * stripe_rows + b * block, block)
            blocks[stripe * block_rows + b, p * piece:(p + 1) * piece, :] = held[p][:, pl.ds(at, block)]
            return carry

        lax.fori_loop(0, block_rows, one, 0, unroll=False)

    def unpack(step, p):
        pl.when(takes_right(step))(lambda: unpack_stripe(p, node - 1 - step))
        pl.when(takes_left(step))(lambda: unpack_stripe(p, node + 1 + step))

    order, near = list(range(1, feats)), feats - 1
    if feats == 4:
        order, near = [2 - odd, 3 - odd, 1 + 2 * odd], 3 - 2 * odd
    split = EARLY * piece

    def exchange(k, low, high):
        peer = lax.rem(feat + k, feats)
        sem = 1 if low > 0 else 0
        return pltpu.make_async_remote_copy(
            agg.at[peer, pl.ds(low, high - low)],
            full.at[pl.ds(pl.multiple_of(feat * width, width) + low, high - low)],
            ex_send.at[k, sem], ex_recv.at[k, sem], device_id={"feat": peer}, device_id_type=MESH,
        )

    def pick(i, steps):
        k = steps[0]
        for at, step in enumerate(steps):
            k = jnp.where(i == at, step, k)
        return k

    def aggregate(k, low, high):
        peer = lax.rem(feat + k, feats)
        sums = []
        for j in range(share):
            r = peer * share + j
            sums.append(lax.dot_general(
                jnp.concatenate([blocks[cols[s, r], low:high, :] for s in range(slots)], axis=1),
                jnp.concatenate([tiles[r, s] for s in range(slots)], axis=1),
                (((1,), (1,)), ((), ())),
                preferred_element_type=jnp.float32,
            ))
        agg[peer, low:high] = jnp.concatenate(sums, axis=1).astype(jnp.bfloat16)

    def far_peers(low, high):
        def turn(i, carry):
            k = pick(i, order[:-1])
            aggregate(k, low, high)
            exchange(k, low, high).start()
            return carry

        if feats > 2:
            lax.fori_loop(0, feats - 2, turn, 0)

    def near_peers():
        def turn(i, carry):
            k = pick(i, [order[-1], 0])
            aggregate(k, 0, width)
            pl.when(i == 0)(lambda: exchange(k, 0, width).start())
            return carry

        lax.fori_loop(0, 2, turn, 0)

    @pl.when(sends_left(0))
    def _():
        for p in range(PIECES):
            left(0, p).start()


    @pl.when(node < nodes - 1)
    def _():
        pl.semaphore_wait(right_in, 1)
        for p in range(PIECES):
            right(0, p).start()

    own = [pltpu.make_async_copy(source(0, p, node), stripe_of(p, node), own_sem.at[p]) for p in range(PIECES)]
    for copy in own:
        copy.start()
    weight_copy = pltpu.make_async_copy(weight_hbm, weight, small_sem.at[1])
    weight_copy.start()
    bias_copy = pltpu.make_async_copy(bias_hbm, bias, small_sem.at[2])
    bias_copy.start()
    cols_copy = pltpu.make_async_copy(cols_hbm, cols, small_sem.at[0])
    cols_copy.start()
    tile_copy = pltpu.make_async_copy(tiles_hbm, tiles, tile_sem)
    tile_copy.start()

    pl.when(node == 0)(meet)
    for step in range(1, nodes - 1):
        for p in range(PIECES):
            @pl.when(sends_left(step))
            def _():
                left(step - 1, p).wait_recv()
                left(step, p).start()

            @pl.when(sends_right(step))
            def _():
                right(step - 1, p).wait_recv()
                right(step, p).start()
    pl.when(node > 0)(meet)
    weight_copy.wait()
    bias_copy.wait()
    column[...] = jnp.broadcast_to(bias[...], (block, bias.shape[1])).T
    for p in range(PIECES):
        own[p].wait()
        unpack_stripe(p, node)
    for step in range(nodes - 2):
        @pl.when(takes_right(step))
        def _():
            for p in range(PIECES):
                pl.when(jnp.logical_not(sends_right(step + 1)))(lambda: right(step, p).wait_recv())
                unpack_stripe(p, node - 1 - step)

        @pl.when(takes_left(step))
        def _():
            for p in range(PIECES):
                pl.when(jnp.logical_not(sends_left(step + 1)))(lambda: left(step, p).wait_recv())
                unpack_stripe(p, node + 1 + step)

    cols_copy.wait()
    tile_copy.wait()
    for p in range(EARLY):
        take(nodes - 2, p)
        unpack(nodes - 2, p)
    far_peers(0, split)
    for p in range(EARLY, PIECES):
        take(nodes - 2, p)
        unpack(nodes - 2, p)
    far_peers(split, width)
    near_peers()

    full[pl.ds(pl.multiple_of(feat * width, width), width), :] = agg[feat]

    for step in range(nodes - 1):
        @pl.when(sends_right(step))
        def _():
            for p in range(PIECES):
                right(step, p).wait_send()

        @pl.when(sends_left(step))
        def _():
            for p in range(PIECES):
                left(step, p).wait_send()

    total = jnp.concatenate([column[...]] * share, axis=1)
    for k in range(1, feats):
        @pl.when(k == near)
        def _():
            exchange(k, 0, width).wait_recv()

        @pl.when(k != near)
        def _():
            exchange(k, 0, split).wait_recv()
            exchange(k, split, width).wait_recv()

    total += jnp.dot(weight[...], full[...], preferred_element_type=jnp.float32)
    out[...] = total.astype(out.dtype)

    for k in range(1, feats):
        @pl.when(k == order[-1])
        def _():
            exchange(k, 0, width).wait_send()

        @pl.when(k != order[-1])
        def _():
            exchange(k, 0, split).wait_send()
            exchange(k, split, width).wait_send()


def on_device(nodes, feats, features, tiles, col_block, weight, bias):
    rows, width = features.shape
    block_rows, _, block, _ = tiles.shape
    share = rows // feats
    classes = weight.shape[1]
    piece = width // PIECES
    logits = pl.pallas_call(
        functools.partial(kernel, nodes, feats),
        out_shape=pltpu.VMEM((classes, share), jnp.bfloat16),
        in_specs=[
            pl.BlockSpec(memory_space=pl.ANY),
            pl.BlockSpec(memory_space=pl.ANY),
            pl.BlockSpec(memory_space=pl.ANY),
            pl.BlockSpec(memory_space=pl.ANY),
            pl.BlockSpec(memory_space=pl.ANY),
        ],
        out_specs=pl.BlockSpec(memory_space=pltpu.VMEM),
        scratch_shapes=[
            pltpu.SMEM(col_block.shape[::-1], col_block.dtype),
            pltpu.VMEM(weight.shape[::-1], weight.dtype),
            pltpu.VMEM((1, classes), bias.dtype),
            pltpu.VMEM((classes, block), bias.dtype),
            pltpu.VMEM(tiles.shape, tiles.dtype),
            pltpu.VMEM((feats, width, share), features.dtype),
            pltpu.VMEM((feats * width, share), features.dtype),
            pltpu.VMEM((nodes * block_rows, width, block), features.dtype),
            pltpu.SemaphoreType.DMA((PIECES,)),
            pltpu.SemaphoreType.DMA,
            pltpu.SemaphoreType.DMA((3,)),
            pltpu.SemaphoreType.DMA((nodes - 1, PIECES)),
            pltpu.SemaphoreType.DMA((nodes - 1, PIECES)),
            pltpu.SemaphoreType.DMA((nodes - 1, PIECES)),
            pltpu.SemaphoreType.DMA((nodes - 1, PIECES)),
            pltpu.SemaphoreType.DMA((feats, 2)),
            pltpu.SemaphoreType.DMA((feats, 2)),
            pltpu.SemaphoreType.REGULAR,
            pltpu.SemaphoreType.REGULAR,
            pltpu.SemaphoreType.REGULAR,
            *[pltpu.VMEM((piece, nodes * rows), features.dtype)] * PIECES,
        ],
        compiler_params=pltpu.CompilerParams(collective_id=0, has_side_effects=True),
    )(col_block.T, features.T, tiles, weight.T, bias[None])
    return logits.T


def solution(mesh):
    in_specs = (
        P(("groups", "node"), "feat"),
        P(("groups", "node"), None, None, None),
        P(("groups", "node"), None),
        P(),
        P(),
    )
    out_specs = P(("groups", "node", "feat"), None)
    body = functools.partial(on_device, mesh.shape["node"], mesh.shape["feat"])
    return jax.shard_map(
        body, mesh=mesh, in_specs=in_specs, out_specs=out_specs, check_vma=False
    )
```

```python
import functools

import jax
import jax.numpy as jnp
from jax import lax
from jax.experimental import pallas as pl
from jax.experimental.pallas import tpu as pltpu
from jax.sharding import PartitionSpec as P

MESH = pl.DeviceIdType.MESH
PIECES = 4
EARLY = 2


def kernel(nodes, feats, cols_hbm, x, tiles_hbm, weight_hbm, bias_hbm, out, cols, weight, bias, column, tiles, agg, full, blocks, own_sem, tile_sem, small_sem, right_send, right_recv, left_send, left_recv,
           ex_send, ex_recv, right_in, above_in, feats_in, *held):
    node = lax.axis_index("node")
    feat = lax.axis_index("feat")
    odd = lax.rem(feat, 2)
    width = x.shape[0]
    piece = width // PIECES
    block_rows, slots, block, _ = tiles.shape
    share = block_rows // feats
    span = share * block
    stripe_rows = block_rows * block
    peers = [lax.rem(feat + k, feats) for k in range(1, feats)]

    barrier = pltpu.get_barrier_semaphore()

    @pl.when(node < nodes - 1)
    def _():
        pl.semaphore_signal(barrier, inc=1, device_id={"node": node + 1}, device_id_type=MESH)

    @pl.when(node == 0)
    def _():
        for peer in peers:
            pl.semaphore_signal(barrier, inc=1, device_id={"feat": peer}, device_id_type=MESH)

    pl.semaphore_wait(barrier, jnp.where(node == 0, feats - 1, 1))

    @pl.when(node > 0)
    def _():
        pl.semaphore_signal(right_in, inc=1, device_id={"node": node - 1}, device_id_type=MESH)

    def meet():
        @pl.when(node > 0)
        def _():
            pl.semaphore_wait(feats_in, 1)

        @pl.when(node < nodes - 1)
        def _():
            for peer in peers:
                pl.semaphore_signal(above_in, inc=1, device_id={"feat": peer}, device_id_type=MESH)
            pl.semaphore_wait(above_in, feats - 1)
            pl.semaphore_signal(feats_in, inc=1, device_id={"node": node + 1}, device_id_type=MESH)

    def stripe_of(p, stripe):
        return held[p].at[:, pl.ds(pl.multiple_of(stripe * stripe_rows, stripe_rows), stripe_rows)]

    def source(step, p, stripe):
        return x.at[pl.ds(p * piece, piece)] if step == 0 else stripe_of(p, stripe)

    def right(step, p):
        stripe = jnp.maximum(node - step, 0)
        return pltpu.make_async_remote_copy(
            source(step, p, stripe), stripe_of(p, stripe), right_send.at[step, p], right_recv.at[step, p],
            device_id={"node": jnp.minimum(node + 1, nodes - 1)}, device_id_type=MESH,
        )

    def left(step, p):
        stripe = jnp.minimum(node + step, nodes - 1)
        return pltpu.make_async_remote_copy(
            source(step, p, stripe), stripe_of(p, stripe), left_send.at[step, p], left_recv.at[step, p],
            device_id={"node": jnp.maximum(node - 1, 0)}, device_id_type=MESH,
        )

    def sends_right(step):
        return jnp.logical_and(node < nodes - 1, node >= step)

    def sends_left(step):
        return jnp.logical_and(node > 0, node + step <= nodes - 1)

    def takes_left(step):
        return node + 1 + step <= nodes - 1

    def takes_right(step):
        return node - 1 - step >= 0

    def take(step, p):
        pl.when(takes_right(step))(lambda: right(step, p).wait_recv())
        pl.when(takes_left(step))(lambda: left(step, p).wait_recv())

    def unpack_stripe(p, stripe):
        def one(b, carry):
            at = pl.multiple_of(stripe * stripe_rows + b * block, block)
            blocks[stripe * block_rows + b, p * piece:(p + 1) * piece, :] = held[p][:, pl.ds(at, block)]
            return carry

        lax.fori_loop(0, block_rows, one, 0, unroll=nodes <= 8)

    def unpack(step, p):
        pl.when(takes_right(step))(lambda: unpack_stripe(p, node - 1 - step))
        pl.when(takes_left(step))(lambda: unpack_stripe(p, node + 1 + step))

    order, near = list(range(1, feats)), feats - 1
    if feats == 4:
        order, near = [2 - odd, 3 - odd, 1 + 2 * odd], 3 - 2 * odd
    split = EARLY * piece

    def exchange(k, low, high):
        peer = lax.rem(feat + k, feats)
        sem = 1 if low > 0 else 0
        return pltpu.make_async_remote_copy(
            agg.at[peer, pl.ds(low, high - low)],
            full.at[pl.ds(pl.multiple_of(feat * width, width) + low, high - low)],
            ex_send.at[k, sem], ex_recv.at[k, sem], device_id={"feat": peer}, device_id_type=MESH,
        )

    def pick(i, steps):
        k = steps[0]
        for at, step in enumerate(steps):
            k = jnp.where(i == at, step, k)
        return k

    def aggregate(k, low, high):
        peer = lax.rem(feat + k, feats)
        sums = []
        for j in range(share):
            r = peer * share + j
            sums.append(lax.dot_general(
                jnp.concatenate([blocks[cols[s, r], low:high, :] for s in range(slots)], axis=1),
                jnp.concatenate([tiles[r, s] for s in range(slots)], axis=1),
                (((1,), (1,)), ((), ())),
                preferred_element_type=jnp.float32,
            ))
        agg[peer, low:high] = jnp.concatenate(sums, axis=1).astype(jnp.bfloat16)

    def far_peers(low, high):
        def turn(i, carry):
            k = pick(i, order[:-1])
            aggregate(k, low, high)
            exchange(k, low, high).start()
            return carry

        if feats > 2:
            lax.fori_loop(0, feats - 2, turn, 0)

    def near_peers():
        def turn(i, carry):
            k = pick(i, [order[-1], 0])
            aggregate(k, 0, width)
            pl.when(i == 0)(lambda: exchange(k, 0, width).start())
            return carry

        lax.fori_loop(0, 2, turn, 0)

    @pl.when(sends_left(0))
    def _():
        for p in range(PIECES):
            left(0, p).start()


    @pl.when(node < nodes - 1)
    def _():
        pl.semaphore_wait(right_in, 1)
        for p in range(PIECES):
            right(0, p).start()

    own = [pltpu.make_async_copy(source(0, p, node), stripe_of(p, node), own_sem.at[p]) for p in range(PIECES)]
    for copy in own:
        copy.start()
    weight_copy = pltpu.make_async_copy(weight_hbm, weight, small_sem.at[1])
    weight_copy.start()
    bias_copy = pltpu.make_async_copy(bias_hbm, bias, small_sem.at[2])
    bias_copy.start()
    cols_copy = pltpu.make_async_copy(cols_hbm, cols, small_sem.at[0])
    cols_copy.start()
    tile_copy = pltpu.make_async_copy(tiles_hbm, tiles, tile_sem)
    tile_copy.start()

    pl.when(node == 0)(meet)
    for step in range(1, nodes - 1):
        for p in range(PIECES):
            @pl.when(sends_left(step))
            def _():
                left(step - 1, p).wait_recv()
                left(step, p).start()

            @pl.when(sends_right(step))
            def _():
                right(step - 1, p).wait_recv()
                right(step, p).start()
    pl.when(node > 0)(meet)
    weight_copy.wait()
    bias_copy.wait()
    column[...] = jnp.broadcast_to(bias[...], (block, bias.shape[1])).T
    for p in range(PIECES):
        own[p].wait()
        unpack_stripe(p, node)
    for step in range(nodes - 2):
        @pl.when(takes_right(step))
        def _():
            for p in range(PIECES):
                pl.when(jnp.logical_not(sends_right(step + 1)))(lambda: right(step, p).wait_recv())
                unpack_stripe(p, node - 1 - step)

        @pl.when(takes_left(step))
        def _():
            for p in range(PIECES):
                pl.when(jnp.logical_not(sends_left(step + 1)))(lambda: left(step, p).wait_recv())
                unpack_stripe(p, node + 1 + step)

    cols_copy.wait()
    tile_copy.wait()
    for p in range(EARLY):
        take(nodes - 2, p)
        unpack(nodes - 2, p)
    far_peers(0, split)
    for p in range(EARLY, PIECES):
        take(nodes - 2, p)
        unpack(nodes - 2, p)
    far_peers(split, width)
    near_peers()

    full[pl.ds(pl.multiple_of(feat * width, width), width), :] = agg[feat]

    for step in range(nodes - 1):
        @pl.when(sends_right(step))
        def _():
            for p in range(PIECES):
                right(step, p).wait_send()

        @pl.when(sends_left(step))
        def _():
            for p in range(PIECES):
                left(step, p).wait_send()

    total = jnp.concatenate([column[...]] * share, axis=1)
    for k in range(1, feats):
        @pl.when(k == near)
        def _():
            exchange(k, 0, width).wait_recv()

        @pl.when(k != near)
        def _():
            exchange(k, 0, split).wait_recv()
            exchange(k, split, width).wait_recv()

    total += jnp.dot(weight[...], full[...], preferred_element_type=jnp.float32)
    out[...] = total.astype(out.dtype)

    for k in range(1, feats):
        @pl.when(k == order[-1])
        def _():
            exchange(k, 0, width).wait_send()

        @pl.when(k != order[-1])
        def _():
            exchange(k, 0, split).wait_send()
            exchange(k, split, width).wait_send()


def on_device(nodes, feats, features, tiles, col_block, weight, bias):
    rows, width = features.shape
    block_rows, _, block, _ = tiles.shape
    share = rows // feats
    classes = weight.shape[1]
    piece = width // PIECES
    logits = pl.pallas_call(
        functools.partial(kernel, nodes, feats),
        out_shape=pltpu.VMEM((classes, share), jnp.bfloat16),
        in_specs=[
            pl.BlockSpec(memory_space=pl.ANY),
            pl.BlockSpec(memory_space=pl.ANY),
            pl.BlockSpec(memory_space=pl.ANY),
            pl.BlockSpec(memory_space=pl.ANY),
            pl.BlockSpec(memory_space=pl.ANY),
        ],
        out_specs=pl.BlockSpec(memory_space=pltpu.VMEM),
        scratch_shapes=[
            pltpu.SMEM(col_block.shape[::-1], col_block.dtype),
            pltpu.VMEM(weight.shape[::-1], weight.dtype),
            pltpu.VMEM((1, classes), bias.dtype),
            pltpu.VMEM((classes, block), bias.dtype),
            pltpu.VMEM(tiles.shape, tiles.dtype),
            pltpu.VMEM((feats, width, share), features.dtype),
            pltpu.VMEM((feats * width, share), features.dtype),
            pltpu.VMEM((nodes * block_rows, width, block), features.dtype),
            pltpu.SemaphoreType.DMA((PIECES,)),
            pltpu.SemaphoreType.DMA,
            pltpu.SemaphoreType.DMA((3,)),
            pltpu.SemaphoreType.DMA((nodes - 1, PIECES)),
            pltpu.SemaphoreType.DMA((nodes - 1, PIECES)),
            pltpu.SemaphoreType.DMA((nodes - 1, PIECES)),
            pltpu.SemaphoreType.DMA((nodes - 1, PIECES)),
            pltpu.SemaphoreType.DMA((feats, 2)),
            pltpu.SemaphoreType.DMA((feats, 2)),
            pltpu.SemaphoreType.REGULAR,
            pltpu.SemaphoreType.REGULAR,
            pltpu.SemaphoreType.REGULAR,
            *[pltpu.VMEM((piece, nodes * rows), features.dtype)] * PIECES,
        ],
        compiler_params=pltpu.CompilerParams(collective_id=0, has_side_effects=True),
    )(col_block.T, features.T, tiles, weight.T, bias[None])
    return logits.T


def solution(mesh):
    in_specs = (
        P(("groups", "node"), "feat"),
        P(("groups", "node"), None, None, None),
        P(("groups", "node"), None),
        P(),
        P(),
    )
    out_specs = P(("groups", "node", "feat"), None)
    body = functools.partial(on_device, mesh.shape["node"], mesh.shape["feat"])
    return jax.shard_map(
        body, mesh=mesh, in_specs=in_specs, out_specs=out_specs, check_vma=False
    )
```

```python
import functools

import jax
import jax.numpy as jnp
from jax import lax
from jax.experimental import pallas as pl
from jax.experimental.pallas import tpu as pltpu
from jax.sharding import PartitionSpec as P

MESH = pl.DeviceIdType.MESH
PIECES = 4
EARLY = 2


def kernel(nodes, feats, cols_hbm, x, tiles_hbm, weight_hbm, bias_hbm, out, cols, weight, bias, column, tiles, agg, full, blocks, own_sem, tile_sem, small_sem, right_send, right_recv, left_send, left_recv,
           ex_send, ex_recv, right_in, above_in, feats_in, partial, *held):
    node = lax.axis_index("node")
    feat = lax.axis_index("feat")
    odd = lax.rem(feat, 2)
    width = x.shape[0]
    piece = width // PIECES
    block_rows, slots, block, _ = tiles.shape
    share = block_rows // feats
    span = share * block
    stripe_rows = block_rows * block
    peers = [lax.rem(feat + k, feats) for k in range(1, feats)]

    barrier = pltpu.get_barrier_semaphore()

    @pl.when(node < nodes - 1)
    def _():
        pl.semaphore_signal(barrier, inc=1, device_id={"node": node + 1}, device_id_type=MESH)

    @pl.when(node == 0)
    def _():
        for peer in peers:
            pl.semaphore_signal(barrier, inc=1, device_id={"feat": peer}, device_id_type=MESH)

    pl.semaphore_wait(barrier, jnp.where(node == 0, feats - 1, 1))

    @pl.when(node > 0)
    def _():
        pl.semaphore_signal(right_in, inc=1, device_id={"node": node - 1}, device_id_type=MESH)

    def meet():
        @pl.when(node > 0)
        def _():
            pl.semaphore_wait(feats_in, 1)

        @pl.when(node < nodes - 1)
        def _():
            for peer in peers:
                pl.semaphore_signal(above_in, inc=1, device_id={"feat": peer}, device_id_type=MESH)
            pl.semaphore_wait(above_in, feats - 1)
            pl.semaphore_signal(feats_in, inc=1, device_id={"node": node + 1}, device_id_type=MESH)

    def stripe_of(p, stripe):
        return held[p].at[:, pl.ds(pl.multiple_of(stripe * stripe_rows, stripe_rows), stripe_rows)]

    def source(step, p, stripe):
        return x.at[pl.ds(p * piece, piece)] if step == 0 else stripe_of(p, stripe)

    def right(step, p):
        stripe = jnp.maximum(node - step, 0)
        return pltpu.make_async_remote_copy(
            source(step, p, stripe), stripe_of(p, stripe), right_send.at[step, p], right_recv.at[step, p],
            device_id={"node": jnp.minimum(node + 1, nodes - 1)}, device_id_type=MESH,
        )

    def left(step, p):
        stripe = jnp.minimum(node + step, nodes - 1)
        return pltpu.make_async_remote_copy(
            source(step, p, stripe), stripe_of(p, stripe), left_send.at[step, p], left_recv.at[step, p],
            device_id={"node": jnp.maximum(node - 1, 0)}, device_id_type=MESH,
        )

    def sends_right(step):
        return jnp.logical_and(node < nodes - 1, node >= step)

    def sends_left(step):
        return jnp.logical_and(node > 0, node + step <= nodes - 1)

    def takes_left(step):
        return node + 1 + step <= nodes - 1

    def takes_right(step):
        return node - 1 - step >= 0

    def take(step, p):
        pl.when(takes_right(step))(lambda: right(step, p).wait_recv())
        pl.when(takes_left(step))(lambda: left(step, p).wait_recv())

    def unpack_stripe(p, stripe):
        def one(b, carry):
            at = pl.multiple_of(stripe * stripe_rows + b * block, block)
            blocks[stripe * block_rows + b, p * piece:(p + 1) * piece, :] = held[p][:, pl.ds(at, block)]
            return carry

        lax.fori_loop(0, block_rows, one, 0, unroll=nodes <= 8)

    def unpack(step, p):
        pl.when(takes_right(step))(lambda: unpack_stripe(p, node - 1 - step))
        pl.when(takes_left(step))(lambda: unpack_stripe(p, node + 1 + step))

    order, near = list(range(1, feats)), feats - 1
    if feats == 4:
        order, near = [2 - odd, 3 - odd, 1 + 2 * odd], 3 - 2 * odd
    split = EARLY * piece

    def exchange(k, low, high):
        peer = lax.rem(feat + k, feats)
        sem = 1 if low > 0 else 0
        return pltpu.make_async_remote_copy(
            agg.at[peer, pl.ds(low, high - low)],
            full.at[pl.ds(pl.multiple_of(feat * width, width) + low, high - low)],
            ex_send.at[k, sem], ex_recv.at[k, sem], device_id={"feat": peer}, device_id_type=MESH,
        )

    def pick(i, steps):
        k = steps[0]
        for at, step in enumerate(steps):
            k = jnp.where(i == at, step, k)
        return k

    def aggregate(k, low, high):
        peer = lax.rem(feat + k, feats)
        sums = []
        for j in range(share):
            r = peer * share + j
            sums.append(lax.dot_general(
                jnp.concatenate([blocks[cols[s, r], low:high, :] for s in range(slots)], axis=1),
                jnp.concatenate([tiles[r, s] for s in range(slots)], axis=1),
                (((1,), (1,)), ((), ())),
                preferred_element_type=jnp.float32,
            ))
        agg[peer, low:high] = jnp.concatenate(sums, axis=1).astype(jnp.bfloat16)

    def far_peers(low, high):
        def turn(i, carry):
            k = pick(i, order[:-1])
            aggregate(k, low, high)
            exchange(k, low, high).start()
            return carry

        if feats > 2:
            lax.fori_loop(0, feats - 2, turn, 0)

    def near_peers():
        def turn(i, carry):
            k = pick(i, [order[-1], 0])
            aggregate(k, 0, width)
            pl.when(i == 0)(lambda: exchange(k, 0, width).start())
            return carry

        lax.fori_loop(0, 2, turn, 0)

    @pl.when(sends_left(0))
    def _():
        for p in range(PIECES):
            left(0, p).start()


    @pl.when(node < nodes - 1)
    def _():
        pl.semaphore_wait(right_in, 1)
        for p in range(PIECES):
            right(0, p).start()

    own = [pltpu.make_async_copy(source(0, p, node), stripe_of(p, node), own_sem.at[p]) for p in range(PIECES)]
    for copy in own:
        copy.start()
    weight_copy = pltpu.make_async_copy(weight_hbm, weight, small_sem.at[1])
    weight_copy.start()
    bias_copy = pltpu.make_async_copy(bias_hbm, bias, small_sem.at[2])
    bias_copy.start()
    cols_copy = pltpu.make_async_copy(cols_hbm, cols, small_sem.at[0])
    cols_copy.start()
    tile_copy = pltpu.make_async_copy(tiles_hbm, tiles, tile_sem)
    tile_copy.start()

    pl.when(node == 0)(meet)
    for step in range(1, nodes - 1):
        for p in range(PIECES):
            @pl.when(sends_left(step))
            def _():
                left(step - 1, p).wait_recv()
                left(step, p).start()

            @pl.when(sends_right(step))
            def _():
                right(step - 1, p).wait_recv()
                right(step, p).start()
    pl.when(node > 0)(meet)
    weight_copy.wait()
    bias_copy.wait()
    column[...] = jnp.broadcast_to(bias[...], (block, bias.shape[1])).T
    for p in range(PIECES):
        own[p].wait()
        unpack_stripe(p, node)
    for step in range(nodes - 2):
        @pl.when(takes_right(step))
        def _():
            for p in range(PIECES):
                pl.when(jnp.logical_not(sends_right(step + 1)))(lambda: right(step, p).wait_recv())
                unpack_stripe(p, node - 1 - step)

        @pl.when(takes_left(step))
        def _():
            for p in range(PIECES):
                pl.when(jnp.logical_not(sends_left(step + 1)))(lambda: left(step, p).wait_recv())
                unpack_stripe(p, node + 1 + step)

    cols_copy.wait()
    tile_copy.wait()
    for p in range(EARLY):
        take(nodes - 2, p)
        unpack(nodes - 2, p)
    far_peers(0, split)
    for p in range(EARLY, PIECES):
        take(nodes - 2, p)
        unpack(nodes - 2, p)
    far_peers(split, width)
    near_peers()

    full[pl.ds(pl.multiple_of(feat * width, width), width), :] = agg[feat]

    for step in range(nodes - 1):
        @pl.when(sends_right(step))
        def _():
            for p in range(PIECES):
                right(step, p).wait_send()

        @pl.when(sends_left(step))
        def _():
            for p in range(PIECES):
                left(step, p).wait_send()

    total = jnp.concatenate([column[...]] * share, axis=1)
    left_over = slice(None)
    if feats == 4:
        exchange(near, 0, width).wait_recv()
        chip = pl.ds(pl.multiple_of((feat - odd) * width, 2 * width), 2 * width)
        left_over = pl.ds(pl.multiple_of((2 - feat + odd) * width, 2 * width), 2 * width)
        partial[...] = total + jnp.dot(weight[:, chip], full[chip, :], preferred_element_type=jnp.float32)
    for k in range(1, feats):
        if feats != 4:
            @pl.when(k == near)
            def _():
                exchange(k, 0, width).wait_recv()

        @pl.when(k != near)
        def _():
            exchange(k, 0, split).wait_recv()
            exchange(k, split, width).wait_recv()

    if feats == 4:
        total = partial[...]
    total += jnp.dot(weight[:, left_over], full[left_over, :], preferred_element_type=jnp.float32)
    out[...] = total.astype(out.dtype)

    for k in range(1, feats):
        @pl.when(k == order[-1])
        def _():
            exchange(k, 0, width).wait_send()

        @pl.when(k != order[-1])
        def _():
            exchange(k, 0, split).wait_send()
            exchange(k, split, width).wait_send()


def on_device(nodes, feats, features, tiles, col_block, weight, bias):
    rows, width = features.shape
    block_rows, _, block, _ = tiles.shape
    share = rows // feats
    classes = weight.shape[1]
    piece = width // PIECES
    logits = pl.pallas_call(
        functools.partial(kernel, nodes, feats),
        out_shape=pltpu.VMEM((classes, share), jnp.bfloat16),
        in_specs=[
            pl.BlockSpec(memory_space=pl.ANY),
            pl.BlockSpec(memory_space=pl.ANY),
            pl.BlockSpec(memory_space=pl.ANY),
            pl.BlockSpec(memory_space=pl.ANY),
            pl.BlockSpec(memory_space=pl.ANY),
        ],
        out_specs=pl.BlockSpec(memory_space=pltpu.VMEM),
        scratch_shapes=[
            pltpu.SMEM(col_block.shape[::-1], col_block.dtype),
            pltpu.VMEM(weight.shape[::-1], weight.dtype),
            pltpu.VMEM((1, classes), bias.dtype),
            pltpu.VMEM((classes, block), bias.dtype),
            pltpu.VMEM(tiles.shape, tiles.dtype),
            pltpu.VMEM((feats, width, share), features.dtype),
            pltpu.VMEM((feats * width, share), features.dtype),
            pltpu.VMEM((nodes * block_rows, width, block), features.dtype),
            pltpu.SemaphoreType.DMA((PIECES,)),
            pltpu.SemaphoreType.DMA,
            pltpu.SemaphoreType.DMA((3,)),
            pltpu.SemaphoreType.DMA((nodes - 1, PIECES)),
            pltpu.SemaphoreType.DMA((nodes - 1, PIECES)),
            pltpu.SemaphoreType.DMA((nodes - 1, PIECES)),
            pltpu.SemaphoreType.DMA((nodes - 1, PIECES)),
            pltpu.SemaphoreType.DMA((feats, 2)),
            pltpu.SemaphoreType.DMA((feats, 2)),
            pltpu.SemaphoreType.REGULAR,
            pltpu.SemaphoreType.REGULAR,
            pltpu.SemaphoreType.REGULAR,
            pltpu.VMEM((classes, share), jnp.float32),
            *[pltpu.VMEM((piece, nodes * rows), features.dtype)] * PIECES,
        ],
        compiler_params=pltpu.CompilerParams(collective_id=0, has_side_effects=True),
    )(col_block.T, features.T, tiles, weight.T, bias[None])
    return logits.T


def solution(mesh):
    in_specs = (
        P(("groups", "node"), "feat"),
        P(("groups", "node"), None, None, None),
        P(("groups", "node"), None),
        P(),
        P(),
    )
    out_specs = P(("groups", "node", "feat"), None)
    body = functools.partial(on_device, mesh.shape["node"], mesh.shape["feat"])
    return jax.shard_map(
        body, mesh=mesh, in_specs=in_specs, out_specs=out_specs, check_vma=False
    )
```

```python
import functools

import jax
import jax.numpy as jnp
from jax import lax
from jax.experimental import pallas as pl
from jax.experimental.pallas import tpu as pltpu
from jax.sharding import PartitionSpec as P

MESH = pl.DeviceIdType.MESH
PIECES = 4
EARLY = 2


def kernel(nodes, feats, cols_hbm, x, tiles_hbm, weight_hbm, bias_hbm, out, cols, weight, bias, column, tiles, agg, full, blocks, own_sem, tile_sem, small_sem, right_send, right_recv, left_send, left_recv,
           ex_send, ex_recv, right_in, above_in, feats_in, *held):
    node = lax.axis_index("node")
    feat = lax.axis_index("feat")
    odd = lax.rem(feat, 2)
    width = x.shape[0]
    piece = width // PIECES
    block_rows, slots, block, _ = tiles.shape
    share = block_rows // feats
    span = share * block
    stripe_rows = block_rows * block
    peers = [lax.rem(feat + k, feats) for k in range(1, feats)]

    barrier = pltpu.get_barrier_semaphore()

    @pl.when(node < nodes - 1)
    def _():
        pl.semaphore_signal(barrier, inc=1, device_id={"node": node + 1}, device_id_type=MESH)

    @pl.when(node == 0)
    def _():
        for peer in peers:
            pl.semaphore_signal(barrier, inc=1, device_id={"feat": peer}, device_id_type=MESH)

    weight_copy = pltpu.make_async_copy(weight_hbm, weight, small_sem.at[1])
    weight_copy.start()
    bias_copy = pltpu.make_async_copy(bias_hbm, bias, small_sem.at[2])
    bias_copy.start()
    cols_copy = pltpu.make_async_copy(cols_hbm, cols, small_sem.at[0])
    cols_copy.start()
    tile_copy = pltpu.make_async_copy(tiles_hbm, tiles, tile_sem)
    tile_copy.start()

    pl.semaphore_wait(barrier, jnp.where(node == 0, feats - 1, 1))

    @pl.when(node > 0)
    def _():
        pl.semaphore_signal(right_in, inc=1, device_id={"node": node - 1}, device_id_type=MESH)

    def meet():
        @pl.when(node > 0)
        def _():
            pl.semaphore_wait(feats_in, 1)

        @pl.when(node < nodes - 1)
        def _():
            for peer in peers:
                pl.semaphore_signal(above_in, inc=1, device_id={"feat": peer}, device_id_type=MESH)
            pl.semaphore_wait(above_in, feats - 1)
            pl.semaphore_signal(feats_in, inc=1, device_id={"node": node + 1}, device_id_type=MESH)

    def stripe_of(p, stripe):
        return held[p].at[:, pl.ds(pl.multiple_of(stripe * stripe_rows, stripe_rows), stripe_rows)]

    def source(step, p, stripe):
        return x.at[pl.ds(p * piece, piece)] if step == 0 else stripe_of(p, stripe)

    def right(step, p):
        stripe = jnp.maximum(node - step, 0)
        return pltpu.make_async_remote_copy(
            source(step, p, stripe), stripe_of(p, stripe), right_send.at[step, p], right_recv.at[step, p],
            device_id={"node": jnp.minimum(node + 1, nodes - 1)}, device_id_type=MESH,
        )

    def left(step, p):
        stripe = jnp.minimum(node + step, nodes - 1)
        return pltpu.make_async_remote_copy(
            source(step, p, stripe), stripe_of(p, stripe), left_send.at[step, p], left_recv.at[step, p],
            device_id={"node": jnp.maximum(node - 1, 0)}, device_id_type=MESH,
        )

    def sends_right(step):
        return jnp.logical_and(node < nodes - 1, node >= step)

    def sends_left(step):
        return jnp.logical_and(node > 0, node + step <= nodes - 1)

    def takes_left(step):
        return node + 1 + step <= nodes - 1

    def takes_right(step):
        return node - 1 - step >= 0

    def take(step, p):
        pl.when(takes_right(step))(lambda: right(step, p).wait_recv())
        pl.when(takes_left(step))(lambda: left(step, p).wait_recv())

    def unpack_stripe(p, stripe):
        def one(b, carry):
            at = pl.multiple_of(stripe * stripe_rows + b * block, block)
            blocks[stripe * block_rows + b, p * piece:(p + 1) * piece, :] = held[p][:, pl.ds(at, block)]
            return carry

        lax.fori_loop(0, block_rows, one, 0, unroll=nodes <= 8)

    def unpack(step, p):
        pl.when(takes_right(step))(lambda: unpack_stripe(p, node - 1 - step))
        pl.when(takes_left(step))(lambda: unpack_stripe(p, node + 1 + step))

    order, near = list(range(1, feats)), feats - 1
    if feats == 4:
        order, near = [2 - odd, 3 - odd, 1 + 2 * odd], 3 - 2 * odd
    split = EARLY * piece

    def exchange(k, low, high):
        peer = lax.rem(feat + k, feats)
        sem = 1 if low > 0 else 0
        return pltpu.make_async_remote_copy(
            agg.at[peer, pl.ds(low, high - low)],
            full.at[pl.ds(pl.multiple_of(feat * width, width) + low, high - low)],
            ex_send.at[k, sem], ex_recv.at[k, sem], device_id={"feat": peer}, device_id_type=MESH,
        )

    def pick(i, steps):
        k = steps[0]
        for at, step in enumerate(steps):
            k = jnp.where(i == at, step, k)
        return k

    def aggregate(k, low, high):
        peer = lax.rem(feat + k, feats)
        sums = []
        for j in range(share):
            r = peer * share + j
            sums.append(lax.dot_general(
                jnp.concatenate([blocks[cols[s, r], low:high, :] for s in range(slots)], axis=1),
                jnp.concatenate([tiles[r, s] for s in range(slots)], axis=1),
                (((1,), (1,)), ((), ())),
                preferred_element_type=jnp.float32,
            ))
        agg[peer, low:high] = jnp.concatenate(sums, axis=1).astype(jnp.bfloat16)

    def far_peers(low, high):
        def turn(i, carry):
            k = pick(i, order[:-1])
            aggregate(k, low, high)
            exchange(k, low, high).start()
            return carry

        if feats > 2:
            lax.fori_loop(0, feats - 2, turn, 0)

    def near_peers():
        def turn(i, carry):
            k = pick(i, [order[-1], 0])
            aggregate(k, 0, width)
            pl.when(i == 0)(lambda: exchange(k, 0, width).start())
            return carry

        lax.fori_loop(0, 2, turn, 0)

    @pl.when(sends_left(0))
    def _():
        for p in range(PIECES):
            left(0, p).start()


    @pl.when(node < nodes - 1)
    def _():
        pl.semaphore_wait(right_in, 1)
        for p in range(PIECES):
            right(0, p).start()

    own = [pltpu.make_async_copy(source(0, p, node), stripe_of(p, node), own_sem.at[p]) for p in range(PIECES)]
    for copy in own:
        copy.start()
    pl.when(node == 0)(meet)
    for step in range(1, nodes - 1):
        for p in range(PIECES):
            @pl.when(sends_left(step))
            def _():
                left(step - 1, p).wait_recv()
                left(step, p).start()

            @pl.when(sends_right(step))
            def _():
                right(step - 1, p).wait_recv()
                right(step, p).start()
    pl.when(node > 0)(meet)
    weight_copy.wait()
    bias_copy.wait()
    column[...] = jnp.broadcast_to(bias[...], (block, bias.shape[1])).T
    for p in range(PIECES):
        own[p].wait()
        unpack_stripe(p, node)
    for step in range(nodes - 2):
        @pl.when(takes_right(step))
        def _():
            for p in range(PIECES):
                pl.when(jnp.logical_not(sends_right(step + 1)))(lambda: right(step, p).wait_recv())
                unpack_stripe(p, node - 1 - step)

        @pl.when(takes_left(step))
        def _():
            for p in range(PIECES):
                pl.when(jnp.logical_not(sends_left(step + 1)))(lambda: left(step, p).wait_recv())
                unpack_stripe(p, node + 1 + step)

    cols_copy.wait()
    tile_copy.wait()
    for p in range(EARLY):
        take(nodes - 2, p)
        unpack(nodes - 2, p)
    far_peers(0, split)
    for p in range(EARLY, PIECES):
        take(nodes - 2, p)
        unpack(nodes - 2, p)
    far_peers(split, width)
    near_peers()

    full[pl.ds(pl.multiple_of(feat * width, width), width), :] = agg[feat]

    for step in range(nodes - 1):
        @pl.when(sends_right(step))
        def _():
            for p in range(PIECES):
                right(step, p).wait_send()

        @pl.when(sends_left(step))
        def _():
            for p in range(PIECES):
                left(step, p).wait_send()

    total = jnp.concatenate([column[...]] * share, axis=1)
    for k in range(1, feats):
        @pl.when(k == near)
        def _():
            exchange(k, 0, width).wait_recv()

        @pl.when(k != near)
        def _():
            exchange(k, 0, split).wait_recv()
            exchange(k, split, width).wait_recv()

    total += jnp.dot(weight[...], full[...], preferred_element_type=jnp.float32)
    out[...] = total.astype(out.dtype)

    for k in range(1, feats):
        @pl.when(k == order[-1])
        def _():
            exchange(k, 0, width).wait_send()

        @pl.when(k != order[-1])
        def _():
            exchange(k, 0, split).wait_send()
            exchange(k, split, width).wait_send()


def on_device(nodes, feats, features, tiles, col_block, weight, bias):
    rows, width = features.shape
    block_rows, _, block, _ = tiles.shape
    share = rows // feats
    classes = weight.shape[1]
    piece = width // PIECES
    logits = pl.pallas_call(
        functools.partial(kernel, nodes, feats),
        out_shape=pltpu.VMEM((classes, share), jnp.bfloat16),
        in_specs=[
            pl.BlockSpec(memory_space=pl.ANY),
            pl.BlockSpec(memory_space=pl.ANY),
            pl.BlockSpec(memory_space=pl.ANY),
            pl.BlockSpec(memory_space=pl.ANY),
            pl.BlockSpec(memory_space=pl.ANY),
        ],
        out_specs=pl.BlockSpec(memory_space=pltpu.VMEM),
        scratch_shapes=[
            pltpu.SMEM(col_block.shape[::-1], col_block.dtype),
            pltpu.VMEM(weight.shape[::-1], weight.dtype),
            pltpu.VMEM((1, classes), bias.dtype),
            pltpu.VMEM((classes, block), bias.dtype),
            pltpu.VMEM(tiles.shape, tiles.dtype),
            pltpu.VMEM((feats, width, share), features.dtype),
            pltpu.VMEM((feats * width, share), features.dtype),
            pltpu.VMEM((nodes * block_rows, width, block), features.dtype),
            pltpu.SemaphoreType.DMA((PIECES,)),
            pltpu.SemaphoreType.DMA,
            pltpu.SemaphoreType.DMA((3,)),
            pltpu.SemaphoreType.DMA((nodes - 1, PIECES)),
            pltpu.SemaphoreType.DMA((nodes - 1, PIECES)),
            pltpu.SemaphoreType.DMA((nodes - 1, PIECES)),
            pltpu.SemaphoreType.DMA((nodes - 1, PIECES)),
            pltpu.SemaphoreType.DMA((feats, 2)),
            pltpu.SemaphoreType.DMA((feats, 2)),
            pltpu.SemaphoreType.REGULAR,
            pltpu.SemaphoreType.REGULAR,
            pltpu.SemaphoreType.REGULAR,
            *[pltpu.VMEM((piece, nodes * rows), features.dtype)] * PIECES,
        ],
        compiler_params=pltpu.CompilerParams(collective_id=0, has_side_effects=True),
    )(col_block.T, features.T, tiles, weight.T, bias[None])
    return logits.T


def solution(mesh):
    in_specs = (
        P(("groups", "node"), "feat"),
        P(("groups", "node"), None, None, None),
        P(("groups", "node"), None),
        P(),
        P(),
    )
    out_specs = P(("groups", "node", "feat"), None)
    body = functools.partial(on_device, mesh.shape["node"], mesh.shape["feat"])
    return jax.shard_map(
        body, mesh=mesh, in_specs=in_specs, out_specs=out_specs, check_vma=False
    )
```
